32 devices in a mesh: mx: 4 (over z), my: 8 (over y, x, core).
Axes of the slice: x: 2, y: 2, z: 4, core: 2. Of those that a mesh axis runs over, the one named last changes fastest.
Arguments:
- noise: bfloat16 [64, 131072], P(None, ('mx', 'my')), may hold values from -6 to 6
- blocks: bfloat16 [2048, 6, 64, 64], P(('mx', 'my')), may hold values from -0.21875 to 0.21875
- pattern: int32 [2048, 6], P(('mx', 'my')), may hold values from 0 to 127
- send_lists: int32 [128, 16], P(('mx', 'my')), may hold values from 0 to 63
- proj_weight: bfloat16 [2048, 2, 64, 128], P(('mx', 'my')), may hold values from -0.0625 to 0.0625
- tile_of: int32 [2048, 2], P(('mx', 'my')), may hold values from 0 to 31, all different within a row
Outputs:
- fields: bfloat16 [64, 131072], P(None, ('mx', 'my'))
- tile_values: float32 [32, 64, 128], P(('mx', 'my'))
The draws below stay inside these ranges and needn't reach their ends.
Inputs may be any that keep to these rules, and one draw needn't show every extreme that they name: `tile_of`: each row names 2 different tiles, and every tile is named by some row.
All inputs are finite; a program needn't handle non-finite values.
Results may differ from the reference program's by a relative error of at most 0.0053.
Values may be sent and summed in bfloat16 or wider, within the bound.
No kernel may reach another device: no remote copies, remote signals or barrier semaphores. Data moves between devices by JAX's collectives and lax.ppermute only.
A program may use at most 128 MiB of HBM per device.

```python
import jax
import jax.numpy as jnp
from jax import lax

FIELDS = 64
BN = 64
K = 6
OV = 2
CELLS = 128
ITERS = 4
TILES_DEV = 1
NBLK = 64
NSEND = 16
NBLK_TOTAL = 2048
NODES = 131072
TILES = 32
N_MX = 4
N_MY = 8


def place_ends(values, stream_key, smallest, largest):
    longest = values.shape.index(max(values.shape))
    spots = []
    for shift in (0, 1):
        where = [jax.random.randint(jax.random.fold_in(stream_key, axis), (), 0, length) for axis, length in enumerate(values.shape)]
        where[longest] = (where[longest] + shift) % values.shape[longest]
        spots.append(tuple(where))
    return values.at[spots[0]].set(smallest).at[spots[1]].set(largest)


def steps_of(rng, extent, pieces, smallest, largest):
    def one(dim, blocks):
        steps = jax.random.uniform(jax.random.fold_in(jax.random.fold_in(rng, 6), dim), (blocks,), jnp.float32, smallest / len(pieces), largest / len(pieces))
        return jnp.repeat(jnp.exp(steps), extent[dim] // blocks).reshape((-1,) + (1,) * (len(extent) - dim - 1))

    gain = one(*pieces[0])
    for cut in pieces[1:]:
        gain = gain * one(*cut)
    return gain


def picks_of(rng, rows, count, top, lift):
    ranking = jax.random.permutation(jax.random.fold_in(rng, 1), count)
    pull = ranking
    for power in range(3):
        pull = pull * pull // count
    pull = pull * lift // count
    tickets = jax.random.randint(jax.random.fold_in(rng, 2), (rows, count), 0, 4096) + pull
    holders = jax.random.permutation(jax.random.fold_in(rng, 3), rows)[jnp.arange(count) % rows]
    tickets = jnp.where(jnp.arange(rows)[:, None] == holders[None, :], 1 << 14, tickets)
    merit = tickets * count + jnp.arange(count)
    return lax.top_k(merit.astype(jnp.int32), top)[1].astype(jnp.int32)


def normal_values(stream_key, extent, scale, reach, split=(), dtype=jnp.bfloat16):
    entries = jax.random.normal(stream_key, extent, jnp.float32) * scale
    if len(split) > 0:
        entries = steps_of(stream_key, extent, split, -0.22, 0.18) * entries
    return jnp.clip(entries, min=-reach, max=reach).astype(dtype)


def setup_inputs(seed: int = 0) -> dict:
    splits = jax.random.split(jax.random.key(seed), 7)
    noise = normal_values(splits[0], (FIELDS, NODES), 1.0, 6.0, ((1, 32),))
    blocks = normal_values(splits[1], (NBLK_TOTAL, K, BN, BN), (2 * K * BN) ** -0.5, 0.21875, ((0, 32),))
    pattern = place_ends(jax.random.randint(splits[2], (NBLK_TOTAL, K), 0, NBLK + 4 * NSEND), jax.random.fold_in(splits[2], 1), 0, (NBLK + 4 * NSEND) - 1).astype(jnp.int32)
    send_lists = place_ends(jax.random.randint(splits[3], (4 * N_MX * N_MY, NSEND), 0, NBLK), jax.random.fold_in(splits[3], 1), 0, NBLK - 1).astype(jnp.int32)
    proj_weight = normal_values(splits[4], (NBLK_TOTAL, OV, BN, CELLS), (BN * NBLK * OV // TILES_DEV) ** -0.5, 0.0625, ((0, 32),))
    tile_of = picks_of(splits[5], NBLK_TOTAL, TILES, OV, 1024)
    return {"noise": noise, "blocks": blocks, "pattern": pattern, "send_lists": send_lists, "proj_weight": proj_weight, "tile_of": tile_of}


COEFFICIENTS = (0.8, 0.6, -0.45, 0.35, -0.3)


def reference(noise, blocks, pattern, send_lists, proj_weight, tile_of):
    devices = N_MX * N_MY
    state = noise.astype(jnp.float32).reshape(FIELDS, devices, NBLK, BN).transpose(1, 0, 2, 3)
    blocks_dev = blocks.reshape(devices, NBLK, K, BN, BN)
    pattern_dev = pattern.reshape(devices, NBLK, K).astype(jnp.int32)
    sends = send_lists.reshape(devices, 4, NSEND).astype(jnp.int32)

    def pick(rounded, lists):
        return jnp.take(rounded, lists, axis=1)

    def apply_one(item):
        extended, pat, blk = item
        columns = jnp.take(extended, pat, axis=1).astype(jnp.float32)
        return jnp.einsum('fbkm,bkmn->fbn', columns, blk.astype(jnp.float32))

    def operate(values):
        rounded = values.astype(jnp.bfloat16)
        payload = jax.vmap(pick)(rounded, sends)
        payload = payload.reshape(N_MX, N_MY, FIELDS, 4, NSEND, BN)
        zero_row = jnp.zeros((1, N_MY, FIELDS, NSEND, BN), jnp.bfloat16)
        zero_col = jnp.zeros((N_MX, 1, FIELDS, NSEND, BN), jnp.bfloat16)
        below = jnp.concatenate([zero_row, payload[:-1, :, :, 0]], axis=0)
        above = jnp.concatenate([payload[1:, :, :, 1], zero_row], axis=0)
        left = jnp.concatenate([zero_col, payload[:, :-1, :, 2]], axis=1)
        right = jnp.concatenate([payload[:, 1:, :, 3], zero_col], axis=1)
        halo = jnp.concatenate([below, above, left, right], axis=3).reshape(devices, FIELDS, 4 * NSEND, BN)
        extended = jnp.concatenate([rounded, halo], axis=2)
        return lax.map(apply_one, (extended, pattern_dev, blocks_dev))

    previous = state
    current = operate(state)
    total = COEFFICIENTS[0] * previous + COEFFICIENTS[1] * current
    for degree in range(2, ITERS + 1):
        following = 2.0 * operate(current) - previous
        total = total + COEFFICIENTS[degree] * following
        previous, current = current, following
    sample = total.astype(jnp.bfloat16)
    fields = sample.transpose(1, 0, 2, 3).reshape(FIELDS, NODES)

    proj_dev = proj_weight.reshape(devices, NBLK, OV, BN, CELLS)
    tiles_dev = tile_of.reshape(devices, NBLK * OV).astype(jnp.int32)

    def accumulate(carry, item):
        part, proj, ids = item
        contrib = jnp.einsum('fbm,bomc->bofc', part.astype(jnp.float32), proj.astype(jnp.float32))
        contrib = contrib.reshape(NBLK * OV, FIELDS * CELLS)
        return carry + jax.ops.segment_sum(contrib, ids, TILES), None

    start = jnp.zeros((TILES, FIELDS * CELLS), jnp.float32)
    summed, _ = lax.scan(accumulate, start, (sample, proj_dev, tiles_dev))
    return fields, summed.reshape(TILES, FIELDS, CELLS)
```

```python
import functools

import jax
import jax.numpy as jnp
from jax import lax
from jax.experimental import pallas as pl
from jax.experimental.pallas import tpu as pltpu
from jax.sharding import PartitionSpec as P

ITERS = 4
COEFFICIENTS = (0.8, 0.6, -0.45, 0.35, -0.3)
VMEM = pl.BlockSpec(memory_space=pltpu.VMEM)
SMEM = pl.BlockSpec(memory_space=pltpu.SMEM)
PARAMS = pltpu.CompilerParams(vmem_limit_bytes=24 << 20)
BF16 = jnp.bfloat16
F32 = jnp.float32


def lower_half(shape, width):
    return lax.broadcasted_iota(jnp.int32, shape, len(shape) - 1) < width


def both_halves(pair, width):
    first, second = pair[:, :width], pair[:, width:]
    return jnp.concatenate([first, first], 1), jnp.concatenate([second, second], 1)


def side_by_side(doubled, one, two, width):
    a, b = doubled[one], doubled[two]
    return jnp.where(lower_half(a.shape, width), a, b)


def fill_payloads(where_ref, sends_ref, doubled, payloads, width):
    for slot, payload in enumerate(payloads):
        row = where_ref[slot]
        for q in range(payload.shape[0]):
            payload[q] = side_by_side(doubled, sends_ref[row, 2 * q], sends_ref[row, 2 * q + 1], width)


def first_kernel(where_ref, sends_ref, noise_ref, doubled, *payloads):
    fields, nodes = noise_ref.shape
    lanes = doubled.shape[2]
    width = lanes // 2
    for q in range(nodes // lanes):
        doubled[2 * q], doubled[2 * q + 1] = both_halves(noise_ref[:, q * lanes : (q + 1) * lanes], width)
    fill_payloads(where_ref, sends_ref, doubled, payloads, width)


def weights_kernel(blocks_ref, out_ref):
    step = pl.program_id(0)
    pairs = blocks_ref.shape[0] // 2
    depth, width = blocks_ref.shape[1:]
    zero = jnp.zeros((depth, width), BF16)
    for r in range(pairs):
        out_ref[step * pairs + r, :depth] = jnp.concatenate([blocks_ref[2 * r], zero], 1)
        out_ref[step * pairs + r, depth:] = jnp.concatenate([zero, blocks_ref[2 * r + 1]], 1)


def unpack_halos(where_ref, halos, doubled, base, width):
    for slot, halo in enumerate(halos):
        count = 2 * halo.shape[0]
        start = base + where_ref[4 + slot] * count
        for q in range(halo.shape[0]):
            doubled[start + 2 * q], doubled[start + 2 * q + 1] = both_halves(halo[q], width)


def applied(pattern_ref, doubled, weights_ref, q, width):
    entries = pattern_ref.shape[0]
    wanted = [pattern_ref[k, 2 * q + side] for side in range(2) for k in range(entries)]
    columns = [side_by_side(doubled, wanted[k], wanted[k + 1], width) for k in range(0, 2 * entries, 2)]
    return jnp.dot(jnp.concatenate(columns, 1), weights_ref[q], preferred_element_type=F32)


def step_kernel(degree, where_ref, sends_ref, pattern_ref, weights_ref, halo_a, halo_b, halo_c, halo_d, *rest):
    if degree == 1:
        noise_ref, _, doubled, current_ref, total_ref, following, *payloads = rest
    else:
        previous_ref, total_in, _, doubled, current_ref, total_ref, following, *payloads = rest
    width = doubled.shape[2] // 2
    lanes = 2 * width
    blocks = pattern_ref.shape[1]
    unpack_halos(where_ref, (halo_a, halo_b, halo_c, halo_d), doubled, blocks, width)

    def body(q, carry):
        product = applied(pattern_ref, doubled, weights_ref, q, width)
        if degree == 1:
            start = noise_ref[:, pl.ds(pl.multiple_of(q * lanes, lanes), lanes)].astype(F32)
            value = product
            total_ref[q] = COEFFICIENTS[0] * start + COEFFICIENTS[1] * value
        else:
            if degree == 2:
                start = previous_ref[:, pl.ds(pl.multiple_of(q * lanes, lanes), lanes)].astype(F32)
            else:
                start = previous_ref[q]
            value = 2.0 * product - start
            total_ref[q] = total_in[q] + COEFFICIENTS[degree] * value
        current_ref[q] = value
        following[2 * q], following[2 * q + 1] = both_halves(value.astype(BF16), width)
        return carry

    lax.fori_loop(0, blocks // 2, body, 0, unroll=4)
    fill_payloads(where_ref, sends_ref, following, payloads, width)


def last_kernel(
    where_ref, pattern_ref, slots_ref, weights_ref, halo_a, halo_b, halo_c, halo_d, previous_ref, total_in, proj_ref, _,
    doubled, fields_ref, sums_ref, send_ref,
):
    width = doubled.shape[2] // 2
    lanes = 2 * width
    blocks = pattern_ref.shape[1]
    unpack_halos(where_ref, (halo_a, halo_b, halo_c, halo_d), doubled, blocks, width)
    sums_ref[...] = jnp.zeros_like(sums_ref)
    count = fields_ref.shape[0]
    cells = proj_ref.shape[3]

    def body(q, carry):
        product = applied(pattern_ref, doubled, weights_ref, q, width)
        value = 2.0 * product - previous_ref[q]
        sample = (total_in[q] + COEFFICIENTS[ITERS] * value).astype(BF16)
        fields_ref[:, pl.ds(pl.multiple_of(q * lanes, lanes), lanes)] = sample
        low = lower_half(sample.shape, width)
        zero = jnp.zeros_like(sample)
        left = jnp.concatenate([jnp.where(low, sample, zero), jnp.where(low, zero, sample)], 0)
        right = jnp.concatenate(
            [jnp.concatenate([proj_ref[2 * q + side, o] for side in range(2)], 0) for o in range(proj_ref.shape[1])], 1
        )
        contribution = jnp.dot(left, right, preferred_element_type=F32)
        for side in range(2):
            for o in range(proj_ref.shape[1]):
                slot = slots_ref[o, 2 * q + side]
                sums_ref[slot] += contribution[side * count : (side + 1) * count, o * cells : (o + 1) * cells]
        return carry

    lax.fori_loop(0, blocks // 2, body, 0, unroll=4)
    half = send_ref.shape[0]
    send_ref[...] = sums_ref[half:].astype(BF16)


def halve_kernel(sums_ref, got_ref, out_ref, send_ref):
    half = got_ref.shape[0]
    out_ref[...] = sums_ref[:half] + got_ref[...].astype(F32)
    send_ref[...] = out_ref[half // 2 :].astype(BF16)


def end_kernel(sums_ref, got_ref, out_ref):
    out_ref[...] = sums_ref[: got_ref.shape[0]] + got_ref[...].astype(F32)


def like(*shape, dtype=BF16):
    return jax.ShapeDtypeStruct(shape, dtype)


def swap_edges(block, axis, odd):
    last = lax.axis_size(axis) - 1
    route = [pair for i in range(odd, last, 2) for pair in ((i, i + 1), (i + 1, i))]
    return lax.ppermute(block, axis, route)


def swap_bit(block, axis, bit):
    return lax.ppermute(block, axis, [(i, i ^ bit) for i in range(lax.axis_size(axis))])


def exchange(payloads):
    (a, b, c, d) = payloads
    return (swap_edges(a, "my", 1), swap_edges(b, "mx", 0), swap_edges(c, "mx", 1), swap_edges(d, "my", 0))


def reversed_bits(value, bits):
    out = value * 0
    for b in range(bits):
        out = out + (((value >> b) & 1) << (bits - 1 - b))
    return out


def shards(noise, blocks, pattern, send_lists, proj_weight, tile_of):
    fields, nodes = noise.shape
    count, entries, width, _ = blocks.shape
    nsend = send_lists.shape[1]
    cells = proj_weight.shape[3]
    rows, cols = lax.axis_size("mx"), lax.axis_size("my")
    devices = rows * cols
    i, j = lax.axis_index("mx"), lax.axis_index("my")
    lanes = 2 * width
    pairs = count // 2

    i_odd, j_odd = i % 2, j % 2
    send_row = [3 - j_odd, i_odd, 1 - i_odd, 2 + j_odd]
    take_row = [2 + j_odd, 1 - i_odd, i_odd, 3 - j_odd]
    where = jnp.stack(send_row + take_row).astype(jnp.int32)
    bits = devices.bit_length() - 1
    slots = reversed_bits(tile_of.T, bits) ^ reversed_bits(i * cols + j, bits)
    pattern = pattern.T
    flat = blocks.reshape(count, entries * width, width)

    extended = like(count + 4 * nsend, fields, lanes)
    payload = [like(nsend // 2, fields, lanes)] * 4
    state = like(pairs, fields, lanes, dtype=F32)

    doubled, *sent = pl.pallas_call(
        first_kernel, out_shape=[extended] + payload, in_specs=[SMEM, SMEM, VMEM], out_specs=[VMEM] * 5, compiler_params=PARAMS,
        name="first",
    )(where, send_lists, noise)
    halos = exchange(sent)
    chunk = min(8, count)
    weights = pl.pallas_call(
        weights_kernel, grid=(count // chunk,), out_shape=like(pairs, 2 * entries * width, lanes),
        in_specs=[pl.BlockSpec((chunk, entries * width, width), lambda g: (g, 0, 0))], out_specs=VMEM, compiler_params=PARAMS,
        name="weights",
    )(flat)
    previous, current, total = None, None, None
    for degree in range(1, ITERS):
        inputs = [where, send_lists, pattern, weights, *halos]
        inputs += [noise] if degree == 1 else [noise if degree == 2 else previous, total]
        inputs += [doubled]
        _, following, total, doubled, *sent = pl.pallas_call(
            functools.partial(step_kernel, degree), out_shape=[extended, state, state, extended] + payload,
            in_specs=[SMEM] * 3 + [VMEM] * (len(inputs) - 3), out_specs=[VMEM] * 8,
            input_output_aliases={len(inputs) - 1: 0}, compiler_params=PARAMS, name=f"step{degree}",
        )(*inputs)
        previous, current = current, following
        halos = exchange(sent)
    inputs = [where, pattern, slots, weights, *halos, previous, total, proj_weight, doubled]
    _, sample, sums, send = pl.pallas_call(
        last_kernel,
        out_shape=[extended, like(fields, nodes), like(devices, fields, cells, dtype=F32), like(devices // 2, fields, cells)],
        in_specs=[SMEM] * 3 + [VMEM] * (len(inputs) - 3), out_specs=[VMEM] * 4,
        input_output_aliases={len(inputs) - 1: 0}, compiler_params=PARAMS, name="last",
    )(*inputs)
    stages = [("my", 1 << b) for b in range(cols.bit_length() - 1)] + [("mx", 1 << b) for b in range(rows.bit_length() - 1)]
    for axis, bit in stages[:-1]:
        got = swap_bit(send, axis, bit)
        half = got.shape[0]
        sums, send = pl.pallas_call(
            halve_kernel, out_shape=[like(half, fields, cells, dtype=F32), like(half // 2, fields, cells)],
            in_specs=[VMEM] * 2, out_specs=[VMEM] * 2, compiler_params=PARAMS, name="halve",
        )(sums, got)
    axis, bit = stages[-1]
    got = swap_bit(send, axis, bit)
    tiles = pl.pallas_call(
        end_kernel, out_shape=like(1, fields, cells, dtype=F32), in_specs=[VMEM] * 2, out_specs=VMEM, compiler_params=PARAMS,
        name="end",
    )(sums, got)
    return sample, tiles


def solution(mesh):
    in_specs = (
        P(None, ("mx", "my")),
        P(("mx", "my"), None, None, None),
        P(("mx", "my"), None),
        P(("mx", "my"), None),
        P(("mx", "my"), None, None, None),
        P(("mx", "my"), None),
    )
    out_specs = (P(None, ("mx", "my")), P(("mx", "my"), None, None))
    return jax.shard_map(shards, mesh=mesh, in_specs=in_specs, out_specs=out_specs, check_vma=False)
```

```python
import functools

import jax
import jax.numpy as jnp
from jax import lax
from jax.experimental import pallas as pl
from jax.experimental.pallas import tpu as pltpu
from jax.sharding import PartitionSpec as P

ITERS = 4
COEFFICIENTS = (0.8, 0.6, -0.45, 0.35, -0.3)
VMEM = pl.BlockSpec(memory_space=pltpu.VMEM)
SMEM = pl.BlockSpec(memory_space=pltpu.SMEM)
PARAMS = pltpu.CompilerParams(vmem_limit_bytes=8 << 20)
BF16 = jnp.bfloat16
F32 = jnp.float32


def lower_half(shape, width):
    return lax.broadcasted_iota(jnp.int32, shape, len(shape) - 1) < width


def both_halves(pair, width):
    first, second = pair[:, :width], pair[:, width:]
    return jnp.concatenate([first, first], 1), jnp.concatenate([second, second], 1)


def side_by_side(doubled, one, two, width):
    a, b = doubled[one], doubled[two]
    return jnp.where(lower_half(a.shape, width), a, b)


def plan():
    i, j = lax.axis_index("mx"), lax.axis_index("my")
    rows, cols = lax.axis_size("mx"), lax.axis_size("my")
    i_odd, j_odd = i & 1, j & 1
    sent = (3 - j_odd, i_odd, 1 - i_odd, 2 + j_odd)
    place = (2 + j_odd, 1 - i_odd, i_odd, 3 - j_odd)
    real = ((j > 0) & (j < cols - 1), None, (i > 0) & (i < rows - 1), None)
    return sent, place, real


def fill_payloads(sends_ref, doubled, payloads, width):
    for row, payload in zip(plan()[0], payloads):
        for q in range(payload.shape[0]):
            payload[q] = side_by_side(doubled, sends_ref[row, 2 * q], sends_ref[row, 2 * q + 1], width)


def first_kernel(sends_ref, noise_ref, doubled, *payloads):
    fields, nodes = noise_ref.shape
    lanes = doubled.shape[2]
    width = lanes // 2
    for q in range(nodes // lanes):
        doubled[2 * q], doubled[2 * q + 1] = both_halves(noise_ref[:, q * lanes : (q + 1) * lanes], width)
    fill_payloads(sends_ref, doubled, payloads, width)


def weights_kernel(blocks_ref, out_ref):
    step = pl.program_id(0)
    pairs = blocks_ref.shape[0] // 2
    depth, width = blocks_ref.shape[1:]
    zero = jnp.zeros((depth, width), BF16)
    for r in range(pairs):
        out_ref[step * pairs + r, :depth] = jnp.concatenate([blocks_ref[2 * r], zero], 1)
        out_ref[step * pairs + r, depth:] = jnp.concatenate([zero, blocks_ref[2 * r + 1]], 1)


def unpack_halos(halos, doubled, base, width):
    _, places, reals = plan()
    for halo, place, real in zip(halos, places, reals):
        count = 2 * halo.shape[0]
        start = base + place * count
        for q in range(halo.shape[0]):
            pair = halo[q]
            if real is not None:
                pair = jnp.where(real, pair, jnp.zeros_like(pair))
            doubled[start + 2 * q], doubled[start + 2 * q + 1] = both_halves(pair, width)


def applied(pattern_ref, doubled, weights_ref, q, width):
    entries = pattern_ref.shape[0]
    wanted = [pattern_ref[k, 2 * q + side] for side in range(2) for k in range(entries)]
    columns = [side_by_side(doubled, wanted[k], wanted[k + 1], width) for k in range(0, 2 * entries, 2)]
    return jnp.dot(jnp.concatenate(columns, 1), weights_ref[q], preferred_element_type=F32)


def step_kernel(degree, sends_ref, pattern_ref, weights_ref, halo_a, halo_b, halo_c, halo_d, *rest):
    if degree == 1:
        noise_ref, _, doubled, current_ref, total_ref, following, *payloads = rest
    else:
        previous_ref, total_in, _, doubled, current_ref, total_ref, following, *payloads = rest
    width = doubled.shape[2] // 2
    lanes = 2 * width
    blocks = pattern_ref.shape[1]
    unpack_halos((halo_a, halo_b, halo_c, halo_d), doubled, blocks, width)

    def body(q, carry):
        product = applied(pattern_ref, doubled, weights_ref, q, width)
        if degree == 1:
            start = noise_ref[:, pl.ds(pl.multiple_of(q * lanes, lanes), lanes)].astype(F32)
            value = product
            total_ref[q] = COEFFICIENTS[0] * start + COEFFICIENTS[1] * value
        else:
            if degree == 2:
                start = previous_ref[:, pl.ds(pl.multiple_of(q * lanes, lanes), lanes)].astype(F32)
            else:
                start = previous_ref[q]
            value = 2.0 * product - start
            total_ref[q] = total_in[q] + COEFFICIENTS[degree] * value
        current_ref[q] = value
        following[2 * q], following[2 * q + 1] = both_halves(value.astype(BF16), width)
        return carry

    lax.fori_loop(0, blocks // 2, body, 0, unroll=16)
    fill_payloads(sends_ref, following, payloads, width)


def last_kernel(
    pattern_ref, tiles_ref, weights_ref, halo_a, halo_b, halo_c, halo_d, previous_ref, total_in, proj_ref, _,
    doubled, fields_ref, sums_ref, send_ref,
):
    width = doubled.shape[2] // 2
    lanes = 2 * width
    blocks = pattern_ref.shape[1]
    unpack_halos((halo_a, halo_b, halo_c, halo_d), doubled, blocks, width)
    sums_ref[...] = jnp.zeros_like(sums_ref)
    count = fields_ref.shape[0]
    cells = proj_ref.shape[3]
    core = lax.axis_index("my") & 1
    half = send_ref.shape[0]

    def body(q, carry):
        product = applied(pattern_ref, doubled, weights_ref, q, width)
        value = 2.0 * product - previous_ref[q]
        sample = (total_in[q] + COEFFICIENTS[ITERS] * value).astype(BF16)
        fields_ref[:, pl.ds(pl.multiple_of(q * lanes, lanes), lanes)] = sample
        low = lower_half(sample.shape, width)
        zero = jnp.zeros_like(sample)
        left = jnp.concatenate([jnp.where(low, sample, zero), jnp.where(low, zero, sample)], 0)
        right = jnp.concatenate(
            [jnp.concatenate([proj_ref[2 * q + side, o] for side in range(2)], 0) for o in range(proj_ref.shape[1])], 1
        )
        contribution = jnp.dot(left, right, preferred_element_type=F32)
        for side in range(2):
            for o in range(proj_ref.shape[1]):
                tile = tiles_ref[o, 2 * q + side]
                slot = ((tile ^ core) & 1) * half + (tile >> 1)
                sums_ref[slot] += contribution[side * count : (side + 1) * count, o * cells : (o + 1) * cells]
        return carry

    lax.fori_loop(0, blocks // 2, body, 0, unroll=16)
    send_ref[...] = sums_ref[half:].astype(BF16)


def join_kernel(sums_ref, got_ref, out_ref):
    out_ref[...] = (sums_ref[: got_ref.shape[0]] + got_ref[...].astype(F32)).astype(BF16)


def end_kernel(parts_ref, out_ref):
    out_ref[0] = jnp.sum(parts_ref[...].astype(F32), axis=0)


def like(*shape, dtype=BF16):
    return jax.ShapeDtypeStruct(shape, dtype)


def swap(block, partner):
    rows, cols = lax.axis_size("mx"), lax.axis_size("my")
    route = []
    for i in range(rows):
        for j in range(cols):
            a, b = partner(i, j)
            route.append((i * cols + j, a * cols + b))
    return lax.ppermute(block, ("mx", "my"), route)


def exchange(payloads):
    rows, cols = lax.axis_size("mx"), lax.axis_size("my")

    def odd_cols(i, j):
        return i, ((j + 1) if j % 2 else (j - 1)) % cols

    def even_rows(i, j):
        return i ^ 1, j

    def odd_rows(i, j):
        if i in (0, rows - 1):
            return i, j ^ 1
        return (i + 1 if i % 2 else i - 1), j

    def even_cols(i, j):
        return i, j ^ 1

    return [swap(block, partner) for block, partner in zip(payloads, (odd_cols, even_rows, odd_rows, even_cols))]


def shards(noise, blocks, pattern, send_lists, proj_weight, tile_of):
    fields, nodes = noise.shape
    count, entries, width, _ = blocks.shape
    nsend = send_lists.shape[1]
    cells = proj_weight.shape[3]
    rows, cols = lax.axis_size("mx"), lax.axis_size("my")
    devices = rows * cols
    lanes = 2 * width
    pairs = count // 2
    pattern = pattern.T
    flat = blocks.reshape(count, entries * width, width)

    extended = like(count + 4 * nsend, fields, lanes)
    payload = [like(nsend // 2, fields, lanes)] * 4
    state = like(pairs, fields, lanes, dtype=F32)

    doubled, *sent = pl.pallas_call(
        first_kernel, out_shape=[extended] + payload, in_specs=[SMEM, VMEM], out_specs=[VMEM] * 5, compiler_params=PARAMS,
        name="first",
    )(send_lists, noise)
    halos = exchange(sent)
    chunk = min(8, count)
    weights = pl.pallas_call(
        weights_kernel, grid=(count // chunk,), out_shape=like(pairs, 2 * entries * width, lanes),
        in_specs=[pl.BlockSpec((chunk, entries * width, width), lambda g: (g, 0, 0))], out_specs=VMEM, compiler_params=PARAMS,
        name="weights",
    )(flat)
    previous, current, total = None, None, None
    for degree in range(1, ITERS):
        inputs = [send_lists, pattern, weights, *halos]
        inputs += [noise] if degree == 1 else [noise if degree == 2 else previous, total]
        inputs += [doubled]
        _, following, total, doubled, *sent = pl.pallas_call(
            functools.partial(step_kernel, degree), out_shape=[extended, state, state, extended] + payload,
            in_specs=[SMEM] * 2 + [VMEM] * (len(inputs) - 2), out_specs=[VMEM] * 8,
            input_output_aliases={len(inputs) - 1: 0}, compiler_params=PARAMS, name=f"step{degree}",
        )(*inputs)
        previous, current = current, following
        halos = exchange(sent)
    inputs = [pattern, tile_of.T, weights, *halos, previous, total, proj_weight, doubled]
    _, sample, sums, send = pl.pallas_call(
        last_kernel,
        out_shape=[extended, like(fields, nodes), like(devices, fields, cells, dtype=F32), like(devices // 2, fields, cells)],
        in_specs=[SMEM] * 2 + [VMEM] * (len(inputs) - 2), out_specs=[VMEM] * 4,
        input_output_aliases={len(inputs) - 1: 0}, compiler_params=PARAMS, name="last",
    )(*inputs)
    got = swap(send, lambda i, j: (i, j ^ 1))
    joined = pl.pallas_call(
        join_kernel, out_shape=like(devices // 2, fields, cells), in_specs=[VMEM] * 2, out_specs=VMEM, compiler_params=PARAMS,
        name="join",
    )(sums, got)
    groups = [[i * cols + j for i in range(rows) for j in range(side, cols, 2)] for side in range(2)]
    parts = lax.all_to_all(joined, ("mx", "my"), 0, 0, tiled=True, axis_index_groups=groups)
    tiles = pl.pallas_call(
        end_kernel, out_shape=like(1, fields, cells, dtype=F32), in_specs=[VMEM], out_specs=VMEM, compiler_params=PARAMS,
        name="end",
    )(parts)
    return sample, tiles


def solution(mesh):
    in_specs = (
        P(None, ("mx", "my")),
        P(("mx", "my"), None, None, None),
        P(("mx", "my"), None),
        P(("mx", "my"), None),
        P(("mx", "my"), None, None, None),
        P(("mx", "my"), None),
    )
    out_specs = (P(None, ("mx", "my")), P(("mx", "my"), None, None))
    return jax.shard_map(shards, mesh=mesh, in_specs=in_specs, out_specs=out_specs, check_vma=False)
```
